32 devices in a mesh: lon: 4 (over x, core), lat: 4 (over z), batch: 2 (over y).
Axes of the slice: x: 2, y: 2, z: 4, core: 2. Of those that a mesh axis runs over, the one named last changes fastest.
Arguments:
- features: bfloat16 [2, 96, 96, 128], P('batch', 'lon', 'lat'), may hold values from -160 to 160
- weight_one: bfloat16 [3, 3, 128, 128], replicated, may hold values from -0.1875 to 0.1875
- norm_gain: float32 [128], replicated, may hold values from 0.1 to 1.9
- norm_bias: float32 [128], replicated, may hold values from -0.6 to 0.6
- weight_two: bfloat16 [3, 3, 128, 128], replicated, may hold values from -0.1875 to 0.1875
- out_cotangent: bfloat16 [2, 96, 96, 128], P('batch', 'lon', 'lat'), may hold values from -0.109375 to 0.109375
Outputs:
- output_maps: bfloat16 [2, 96, 96, 128], P('batch', 'lon', 'lat')
- grad_one: float32 [3, 3, 128, 128], replicated
- grad_two: float32 [3, 3, 128, 128], replicated
- grad_gain: float32 [128], replicated
- grad_bias: float32 [128], replicated
The draws below stay inside these ranges and needn't reach their ends.
All inputs are finite; a program needn't handle non-finite values.
Results may differ from the reference program's by a relative error of at most 0.005.
Values may be sent and summed in bfloat16 or wider, within the bound.
No kernel may reach another device: no remote copies, remote signals or barrier semaphores. Data moves between devices by JAX's collectives and lax.ppermute only.
A program may use at most 64 MiB of HBM per device.

```python
import jax
import jax.numpy as jnp
from jax import lax

C = 128
RATE_ONE = 6
RATE_TWO = 12
S_DEV = 1
NLON = 96
NLAT = 96
SAMPLES = 2


def draw_features(key, part):
    key_chan = jax.random.fold_in(key, 11)
    key_base = jax.random.fold_in(key, 12)
    chan = jnp.exp(jax.random.uniform(key_chan, (C,), jnp.float32) * jnp.log(10.0)) / 3.0
    lon_pos = jnp.arange(NLON, dtype=jnp.float32) / (NLON - 1)
    lat_pos = jnp.arange(NLAT, dtype=jnp.float32) / (NLAT - 1)
    base = jax.random.truncated_normal(key_base, -5.0, 5.0, (SAMPLES, NLON, NLAT, C), jnp.float32)
    lon_scale = 3.0 ** lon_pos
    lat_scale = 1.5 ** lat_pos
    return (base * chan * lon_scale[None, :, None, None] * lat_scale[None, None, :, None]).astype(jnp.bfloat16)


def level_of(key, shape, split, least, high):
    factor_of, own = 1.0, jax.random.fold_in(key, 6)
    for position, blocks in split:
        draws = jnp.exp(jax.random.uniform(jax.random.fold_in(own, position), (blocks,), jnp.float32, least / len(split), high / len(split)))
        factor_of = factor_of * jnp.repeat(draws, shape[position] // blocks).reshape([-1 if axis == position else 1 for axis in range(len(shape))])
    return factor_of


def normal_values(rng, shape, spread, reach, cuts=(), kind=jnp.bfloat16):
    loudness = level_of(rng, shape, cuts, -0.22, 0.18) if cuts else 1.0
    entries = jax.random.normal(rng, shape, jnp.float32) * spread * loudness
    return jnp.minimum(jnp.maximum(entries, -reach), reach).astype(kind)


def setup_inputs(seed: int = 0) -> dict:
    splits = jax.random.split(jax.random.key(seed), 7)
    return {
        "features": draw_features(jax.random.fold_in(splits[6], 71), 0),
        "weight_one": normal_values(splits[1], (3, 3, C, C), (9 * C) ** -0.5, 0.1875),
        "norm_gain": jnp.clip(1.0 + 0.18 * jax.random.normal(splits[2], (C,), jnp.float32), 0.1, 1.9),
        "norm_bias": jnp.clip(jax.random.uniform(splits[3], (C,), jnp.float32, -0.6, 0.6), -0.6, 0.6),
        "weight_two": normal_values(splits[4], (3, 3, C, C), (9 * C) ** -0.5, 0.1875),
        "out_cotangent": normal_values(splits[5], (SAMPLES, NLON, NLAT, C), ((SAMPLES * NLON * NLAT) ** -0.5), 0.109375, ((0, 2), (1, 4), (2, 4))),
    }


HIGH = lax.Precision.HIGHEST

def extend(field, rate):
    wrapped = jnp.concatenate([field[:, -rate:], field, field[:, :rate]], axis=1)
    return jnp.pad(wrapped, ((0, 0), (0, 0), (rate, rate), (0, 0)))

def conv_apply(field, kernel, rate):
    return lax.conv_general_dilated(extend(field, rate), kernel, (1, 1), 'VALID', rhs_dilation=(rate, rate), dimension_numbers=('NHWC', 'HWIO', 'NHWC'), precision=HIGH)

def kernel_grad(field, grad, rate):
    padded = extend(field, rate)
    rows, cols = (grad.shape[1], grad.shape[2])
    result = []
    for first in range(3):
        line = []
        for second in range(3):
            window = padded[:, first * rate:first * rate + rows, second * rate:second * rate + cols]
            line.append(jnp.einsum('spqc,spqo->co', window, grad, precision=HIGH))
        result.append(jnp.stack(line))
    return jnp.stack(result)

def reference(features, weight_one, norm_gain, norm_bias, weight_two, out_cotangent):
    w_one = weight_one.astype(jnp.float32)
    w_two = weight_two.astype(jnp.float32)
    flipped = jnp.flip(w_two, (0, 1)).transpose(0, 1, 3, 2)
    count = S_DEV * NLON * NLAT
    groups = SAMPLES // S_DEV
    feats = features.reshape(groups, S_DEV, NLON, NLAT, C)
    cotan = out_cotangent.reshape(groups, S_DEV, NLON, NLAT, C)

    def group(pair):
        xin, gout = pair
        xf = xin.astype(jnp.float32)
        pre_one = conv_apply(xf, w_one, RATE_ONE)
        mean = lax.optimization_barrier(jnp.sum(pre_one, axis=(0, 1, 2))) / count
        var = lax.optimization_barrier(jnp.sum((pre_one - mean) ** 2, axis=(0, 1, 2))) / count
        rstd = lax.rsqrt(var + 1e-05)
        normed = (pre_one - mean) * rstd
        shifted = norm_gain * normed + norm_bias
        sig = jax.nn.sigmoid(shifted)
        hidden = (shifted * sig).astype(jnp.bfloat16)
        hf = hidden.astype(jnp.float32)
        output = conv_apply(hf, w_two, RATE_TWO).astype(jnp.bfloat16)
        gf = gout.astype(jnp.float32)
        grad_hidden = conv_apply(gf, flipped, RATE_TWO)
        grad_shift = grad_hidden * sig * (1.0 + shifted * (1.0 - sig))
        sum_b = lax.optimization_barrier(jnp.sum(grad_shift, axis=(0, 1, 2)))
        sum_ba = lax.optimization_barrier(jnp.sum(grad_shift * normed, axis=(0, 1, 2)))
        grad_pre = ((norm_gain * grad_shift - norm_gain * sum_b / count - normed * norm_gain * sum_ba / count) * rstd).astype(jnp.bfloat16)
        g_two = kernel_grad(hf, gf, RATE_TWO)
        g_one = kernel_grad(xf, grad_pre.astype(jnp.float32), RATE_ONE)
        return (output, g_one, g_two, sum_b, sum_ba)
    output, g_one, g_two, sum_b, sum_ba = lax.map(group, (feats, cotan))
    output_maps = output.reshape(SAMPLES, NLON, NLAT, C)
    return (output_maps, lax.optimization_barrier(jnp.sum(g_one, 0)), lax.optimization_barrier(jnp.sum(g_two, 0)), lax.optimization_barrier(jnp.sum(sum_ba, 0)), lax.optimization_barrier(jnp.sum(sum_b, 0)))
```

```python
import jax
import jax.numpy as jnp
from jax import lax
from jax.sharding import PartitionSpec as P

RATE_ONE = 6
RATE_TWO = 12
TILE = ("lon", "lat")
EVERY = ("lon", "lat", "batch")


def extended(value, sides, width, wrap):
    for axis, dim in sides:
        devices, length = (lax.axis_size(axis), value.shape[dim])
        up = [(i, (i + 1) % devices) for i in range(devices if wrap else devices - 1)]
        down = [(j, i) for i, j in up]
        last = lax.slice_in_dim(value, length - width, length, axis=dim)
        initial = lax.slice_in_dim(value, 0, width, axis=dim)
        before = lax.ppermute(last, axis, up)
        after = lax.ppermute(initial, axis, down)
        value = jnp.concatenate([before, value, after], axis=dim)
    return value


def extend(field, width):
    wide = extended(field, (("lon", 1),), width, True)
    return extended(wide, (("lat", 2),), width, False)


def conv_valid(padded, kernel, rate):
    return lax.conv_general_dilated(
        padded,
        kernel,
        (1, 1),
        "VALID",
        rhs_dilation=(rate, rate),
        dimension_numbers=("NHWC", "HWIO", "NHWC"),
        preferred_element_type=jnp.float32,
    )


def windows(padded, rate, rows, cols):
    return [
        padded[:, a * rate : a * rate + rows, b * rate : b * rate + cols].reshape(-1, padded.shape[3])
        for a in range(3)
        for b in range(3)
    ]


def outer(left, right):
    return lax.dot_general(left, right, (((0,), (0,)), ((), ())), preferred_element_type=jnp.float32)


def gathered(value, axes):
    members = lax.axis_size(axes)
    copies = jnp.broadcast_to(value[None], (members,) + value.shape)
    return lax.all_to_all(copies, axes, 0, 0)


def summed(parts):
    lon, lat, batch = (lax.axis_size(a) for a in EVERY)
    pairs = [(i, i ^ 1) for i in range(lon)]
    core = lax.axis_index("lon") % 2
    groups = [
        [((x * 2 + c) * lat + z) * batch + y for x in range(lon // 2) for z in range(lat) for y in range(batch)]
        for c in range(2)
    ]
    members = lon // 2 * lat * batch
    sent = lax.dynamic_index_in_dim(parts, 1 - core, 0, keepdims=False).astype(jnp.bfloat16)
    kept = lax.dynamic_index_in_dim(parts, core, 0, keepdims=False)
    half = kept + lax.ppermute(sent, "lon", pairs).astype(jnp.float32)
    rows = half.shape[0]
    chunk = -(-rows // (members * 8)) * 8
    half = jnp.pad(half.astype(jnp.bfloat16), ((0, chunk * members - rows), (0, 0)))
    chunks = lax.all_to_all(half.reshape(members, chunk, -1), EVERY, 0, 0, axis_index_groups=groups)
    own = jnp.sum(chunks.astype(jnp.float32), axis=0).astype(jnp.bfloat16)
    copies = jnp.broadcast_to(own[None], (members,) + own.shape)
    whole = lax.all_to_all(copies, EVERY, 0, 0, axis_index_groups=groups)
    mine = whole.reshape(members * chunk, -1)[:rows]
    other = lax.ppermute(mine, "lon", pairs)
    first = jnp.where(core == 0, mine, other).astype(jnp.float32)
    second = jnp.where(core == 0, other, mine).astype(jnp.float32)
    return first, second


def local(features, weight_one, norm_gain, norm_bias, weight_two, out_cotangent):
    cells = features.shape[0] * features.shape[1] * features.shape[2]
    count = cells * lax.axis_size(TILE)
    rows, cols = features.shape[1:3]
    feats_wide = extend(features, RATE_ONE)
    pre_one = conv_valid(feats_wide, weight_one, RATE_ONE)
    near = jnp.sum(pre_one, axis=(0, 1, 2)) / cells
    around = jnp.sum((pre_one - near) ** 2, axis=(0, 1, 2))
    stats = gathered(jnp.stack([near, around]), TILE)
    mean = jnp.mean(stats[:, 0], axis=0)
    var = (jnp.sum(stats[:, 1], axis=0) + cells * jnp.sum((stats[:, 0] - mean) ** 2, axis=0)) / count
    rstd = lax.rsqrt(var + 1e-05)
    normed = (pre_one - mean) * rstd
    shifted = norm_gain * normed + norm_bias
    sig = jax.nn.sigmoid(shifted)
    hidden = (shifted * sig).astype(jnp.bfloat16)
    cotan_wide = extend(out_cotangent, RATE_TWO)
    flipped = jnp.flip(weight_two, (0, 1)).transpose(0, 1, 3, 2)
    grad_hidden = conv_valid(cotan_wide, flipped, RATE_TWO)
    grad_shift = grad_hidden * sig * (1.0 + shifted * (1.0 - sig))
    local_b = jnp.sum(grad_shift, axis=(0, 1, 2))
    local_ba = jnp.sum(grad_shift * normed, axis=(0, 1, 2))
    every = gathered(jnp.stack([local_b, local_ba]), EVERY)
    every = every.reshape(-1, lax.axis_size("batch"), 2, every.shape[-1])
    group = jnp.sum(every, axis=0)
    sum_b, sum_ba = lax.dynamic_index_in_dim(group, lax.axis_index("batch"), 0, keepdims=False)
    grad_bias, grad_gain = jnp.sum(group, axis=0)
    grad_pre = (
        (norm_gain * grad_shift - norm_gain * sum_b / count - normed * norm_gain * sum_ba / count)
        * rstd
    ).astype(jnp.bfloat16)
    hidden_wide = extend(hidden, RATE_TWO)
    output_maps = conv_valid(hidden_wide, weight_two, RATE_TWO).astype(jnp.bfloat16)
    hidden_rows = hidden.reshape(cells, -1)
    grad_rows = grad_pre.reshape(cells, -1)
    part_two = jnp.concatenate([outer(hidden_rows, w) for w in reversed(windows(cotan_wide, RATE_TWO, rows, cols))])
    part_one = jnp.concatenate([outer(w, grad_rows) for w in windows(feats_wide, RATE_ONE, rows, cols)])
    grad_one, grad_two = summed(jnp.stack([part_one, part_two]))
    shape = weight_one.shape
    return (output_maps, grad_one.reshape(shape), grad_two.reshape(shape), grad_gain, grad_bias)


def solution(mesh):
    placed = (P("batch", "lon", "lat", None), P(), P(), P(), P(), P("batch", "lon", "lat", None))
    return jax.shard_map(
        local,
        mesh=mesh,
        in_specs=placed,
        out_specs=(P("batch", "lon", "lat", None), P(), P(), P(), P()),
        check_vma=False,
    )
```

```python
import jax
import jax.numpy as jnp
from jax import lax
from jax.experimental import pallas as pl
from jax.experimental.pallas import tpu as pltpu
from jax.sharding import PartitionSpec as P

RATE_ONE = 6
RATE_TWO = 12
TILE = ("lon", "lat")
EVERY = ("lon", "lat", "batch")
TAPS = [(a, b) for a in range(3) for b in range(3)]
LIMIT = 32 * 1024 * 1024


def swapped(first, last, axis, wrap):
    devices = lax.axis_size(axis)
    odd = lax.axis_index(axis) % 2 == 1
    near = [(i, i ^ 1) for i in range(devices)]
    far = [(i, (i + 1 if i % 2 else i - 1) % devices) for i in range(devices)]
    if not wrap:
        far = [(i, j) for i, j in far if abs(i - j) == 1]
    one = lax.ppermute(jnp.where(odd, first, last), axis, near)
    two = lax.ppermute(jnp.where(odd, last, first), axis, far)
    return jnp.where(odd, one, two), jnp.where(odd, two, one)


def along_lon(tile, width):
    before, after = swapped(tile[:width], tile[-width:], "lon", True)
    return jnp.concatenate([before, tile, after])


def along_lat(tall, width):
    cols = tall.shape[1]
    before, after = swapped(tall[:, :width], tall[:, -width:], "lat", False)
    down = jnp.concatenate([before, tall[:, : cols - width]], axis=1)
    up = jnp.concatenate([tall[:, width:], after], axis=1)
    return [s.reshape(-1, s.shape[2]) for s in (down, tall, up)]


def call(body, outs, flops, *args):
    moved = sum(a.size * a.dtype.itemsize for a in args) + sum(o.size * o.dtype.itemsize for o in outs)
    return pl.pallas_call(
        body,
        out_shape=outs,
        compiler_params=pltpu.CompilerParams(vmem_limit_bytes=LIMIT),
        cost_estimate=pl.CostEstimate(flops=flops, bytes_accessed=moved, transcendentals=0),
    )(*args)


def shaped(rows, channels, kind=jnp.float32):
    return jax.ShapeDtypeStruct((rows, channels), kind)


def dot(left, right, over):
    return lax.dot_general(left, right, ((over[:1], over[1:]), ((), ())), preferred_element_type=jnp.float32)


def convolved(shifts, weight, step, cells, flip):
    total = None
    for a, b in TAPS:
        kernel = weight[2 - a, 2 - b] if flip else weight[a, b]
        term = dot(shifts[b][a * step : a * step + cells, :], kernel, (1, 1) if flip else (1, 0))
        total = term if total is None else total + term
    return total


def local(features, weight_one, norm_gain, norm_bias, weight_two, out_cotangent):
    _, rows, cols, channels = features.shape
    cells = rows * cols
    count = cells * lax.axis_size(TILE)
    step_one, step_two = RATE_ONE * cols, RATE_TWO * cols
    work = 2 * 9 * cells * channels * channels
    gain, bias = norm_gain[None], norm_bias[None]

    feats_tall = along_lon(features[0], RATE_ONE)
    cotan_tall = along_lon(out_cotangent[0], RATE_TWO)
    feats = along_lat(feats_tall, RATE_ONE)

    def first_conv(s0, s1, s2, weight, pre_ref, stat_ref):
        pre = convolved((s0, s1, s2), weight, step_one, cells, False)
        near = jnp.sum(pre, axis=0, keepdims=True) * (1.0 / cells)
        around = jnp.sum((pre - near) ** 2, axis=0, keepdims=True)
        pre_ref[...] = pre
        stat_ref[...] = jnp.concatenate([near, around])

    pre_one, stat = call(first_conv, [shaped(cells, channels), shaped(2, channels)], work, *feats, weight_one)
    members = lax.axis_size(TILE)
    stats = lax.all_to_all(jnp.broadcast_to(stat[None], (members, 2, channels)), TILE, 0, 0)

    cotan = along_lat(cotan_tall, RATE_TWO)

    def cotangent_conv(c0, c1, c2, weight, out_ref):
        out_ref[...] = convolved((c0, c1, c2), weight, step_two, cells, True)

    (grad_hidden,) = call(cotangent_conv, [shaped(cells, channels)], work, *cotan, weight_two)

    def activate(stats, pre, grad, gain, bias, hidden_ref, shift_ref, normed_ref, rstd_ref, sums_ref):
        means = stats[:, 0, :]
        mean = jnp.sum(means, axis=0, keepdims=True) * (1.0 / members)
        apart = jnp.sum((means - mean) ** 2, axis=0, keepdims=True)
        var = (jnp.sum(stats[:, 1, :], axis=0, keepdims=True) + cells * apart) * (1.0 / count)
        rstd = lax.rsqrt(var + 1e-05)
        normed = (pre[...] - mean) * rstd
        shifted = gain[...] * normed + bias[...]
        sig = 1.0 / (1.0 + jnp.exp(-shifted))
        hidden_ref[...] = (shifted * sig).astype(jnp.bfloat16)
        shift = grad[...] * sig * (1.0 + shifted * (1.0 - sig))
        shift_ref[...] = shift
        normed_ref[...] = normed
        rstd_ref[...] = rstd
        sum_b = jnp.sum(shift, axis=0, keepdims=True)
        sum_ba = jnp.sum(shift * normed, axis=0, keepdims=True)
        sums_ref[...] = jnp.concatenate([sum_b, sum_ba])

    hidden, grad_shift, normed, rstd, sums = call(
        activate,
        [
            shaped(cells, channels, jnp.bfloat16),
            shaped(cells, channels),
            shaped(cells, channels),
            shaped(1, channels),
            shaped(2, channels),
        ],
        cells * channels * 20,
        stats, pre_one, grad_hidden, gain, bias,
    )
    devices = lax.axis_size(EVERY)
    batches = lax.axis_size("batch")
    every = lax.all_to_all(jnp.broadcast_to(sums[None], (devices, 2, channels)), EVERY, 0, 0)
    group = jnp.sum(every.reshape(-1, batches, 2, channels), axis=0)
    grad_bias, grad_gain = jnp.sum(group, axis=0)
    own = lax.dynamic_index_in_dim(group, lax.axis_index("batch"), 0, keepdims=False)

    hidden_tall = along_lon(hidden.reshape(rows, cols, channels), RATE_TWO)
    hiddens = along_lat(hidden_tall, RATE_TWO)

    def second_conv(h0, h1, h2, weight, out_ref):
        out_ref[...] = convolved((h0, h1, h2), weight, step_two, cells, False).astype(jnp.bfloat16)

    def second_grad(hidden, c0, c1, c2, out_ref):
        for n, (a, b) in enumerate(TAPS):
            window = (c0, c1, c2)[2 - b][(2 - a) * step_two : (2 - a) * step_two + cells, :]
            out_ref[n * channels : (n + 1) * channels, :] = dot(hidden[...], window, (0, 0)).astype(jnp.bfloat16)

    part_shape = shaped(9 * channels, channels, jnp.bfloat16)
    (part_two,) = call(second_grad, [part_shape], work, hidden, *cotan)

    def first_grad(own, shift, normed, gain, rstd, s0, s1, s2, out_ref):
        scale = gain[...] * rstd[...]
        base = own[0:1, :] * (1.0 / count)
        slope = own[1:2, :] * (1.0 / count)
        grad = ((shift[...] - base - normed[...] * slope) * scale).astype(jnp.bfloat16)
        for n, (a, b) in enumerate(TAPS):
            window = (s0, s1, s2)[b][a * step_one : a * step_one + cells, :]
            out_ref[n * channels : (n + 1) * channels, :] = dot(window, grad, (0, 0)).astype(jnp.bfloat16)

    (part_one,) = call(first_grad, [part_shape], work, own, grad_shift, normed, gain, rstd, *feats)

    lon, lat, batch = (lax.axis_size(a) for a in EVERY)
    pairs = [(i, i ^ 1) for i in range(lon)]
    core = lax.axis_index("lon") % 2 == 1
    groups = [
        [((x * 2 + c) * lat + z) * batch + y for x in range(lon // 2) for z in range(lat) for y in range(batch)]
        for c in range(2)
    ]
    size = devices // 2
    total = 9 * channels
    chunk = -(-total // (size * 8)) * 8
    sent = jnp.where(core, part_one, part_two)
    kept = jnp.where(core, part_two, part_one)
    half = (kept.astype(jnp.float32) + lax.ppermute(sent, "lon", pairs).astype(jnp.float32)).astype(jnp.bfloat16)
    half = jnp.pad(half, ((0, chunk * size - total), (0, 0)))
    chunks = lax.all_to_all(half.reshape(size, chunk, channels), EVERY, 0, 0, axis_index_groups=groups)
    piece = jnp.sum(chunks.astype(jnp.float32), axis=0).astype(jnp.bfloat16)
    whole = lax.all_to_all(
        jnp.broadcast_to(piece[None], (size, chunk, channels)), EVERY, 0, 0, axis_index_groups=groups
    )
    (maps,) = call(second_conv, [shaped(cells, channels, jnp.bfloat16)], work, *hiddens, weight_two)
    mine = whole.reshape(size * chunk, channels)[:total]
    other = lax.ppermute(mine, "lon", pairs)
    shape = weight_one.shape
    grad_one = jnp.where(core, other, mine).astype(jnp.float32).reshape(shape)
    grad_two = jnp.where(core, mine, other).astype(jnp.float32).reshape(shape)
    return (maps.reshape(features.shape), grad_one, grad_two, grad_gain, grad_bias)


def solution(mesh):
    placed = (P("batch", "lon", "lat", None), P(), P(), P(), P(), P("batch", "lon", "lat", None))
    return jax.shard_map(
        local,
        mesh=mesh,
        in_specs=placed,
        out_specs=(P("batch", "lon", "lat", None), P(), P(), P(), P()),
        check_vma=False,
    )
```

```python
import jax
import jax.numpy as jnp
from jax import lax
from jax.experimental import pallas as pl
from jax.experimental.pallas import tpu as pltpu
from jax.sharding import PartitionSpec as P


RATE_ONE = 6
RATE_TWO = 12
TILE = ("lon", "lat")
EVERY = ("lon", "lat", "batch")
TAPS = [(a, b) for a in range(3) for b in range(3)]
LIMIT = 32 * 1024 * 1024


def swapped(first, last, axis, wrap):
    devices = lax.axis_size(axis)
    odd = lax.axis_index(axis) % 2 == 1
    near = [(i, i ^ 1) for i in range(devices)]
    far = [(i, (i + 1 if i % 2 else i - 1) % devices) for i in range(devices)]
    if not wrap:
        far = [(i, j) for i, j in far if abs(i - j) == 1]
    one = lax.ppermute(jnp.where(odd, first, last), axis, near)
    two = lax.ppermute(jnp.where(odd, last, first), axis, far)
    return jnp.where(odd, one, two), jnp.where(odd, two, one)


def widened(tile, width, axis):
    dim = ("lon", "lat").index(axis)
    length = tile.shape[dim]
    first = lax.slice_in_dim(tile, 0, width, axis=dim)
    last = lax.slice_in_dim(tile, length - width, length, axis=dim)
    before, after = swapped(first, last, axis, axis == "lon")
    return jnp.concatenate([before, tile, after], axis=dim)


def shifts(wide, width):
    cols = wide.shape[1] - 2 * width
    return [wide[:, b * width : b * width + cols].reshape(-1, wide.shape[2]) for b in range(3)]


def shifted_copies(tile, width, order):
    for axis in order:
        tile = widened(tile, width, axis)
    return shifts(tile, width)


def call(body, outs, flops, *args):
    moved = sum(a.size * a.dtype.itemsize for a in args) + sum(o.size * o.dtype.itemsize for o in outs)
    return pl.pallas_call(
        body,
        out_shape=outs,
        compiler_params=pltpu.CompilerParams(vmem_limit_bytes=LIMIT),
        cost_estimate=pl.CostEstimate(flops=flops, bytes_accessed=moved, transcendentals=0),
    )(*args)


def shaped(rows, channels, kind=jnp.float32):
    return jax.ShapeDtypeStruct((rows, channels), kind)


def dot(left, right, over):
    return lax.dot_general(left, right, ((over[:1], over[1:]), ((), ())), preferred_element_type=jnp.float32)


def convolved(shifts, weight, step, cells, flip):
    total = None
    for a, b in TAPS:
        kernel = weight[2 - a, 2 - b] if flip else weight[a, b]
        term = dot(shifts[b][a * step : a * step + cells, :], kernel, (1, 1) if flip else (1, 0))
        total = term if total is None else total + term
    return total


def local(features, weight_one, norm_gain, norm_bias, weight_two, out_cotangent):
    _, rows, cols, channels = features.shape
    cells = rows * cols
    count = cells * lax.axis_size(TILE)
    step_one, step_two = RATE_ONE * cols, RATE_TWO * cols
    work = 2 * 9 * cells * channels * channels

    def stage(w1, w2, gain, bias, w1_ref, w2_ref, gain_ref, bias_ref):
        w1_ref[...] = w1[...]
        w2_ref[...] = w2[...]
        gain_ref[...] = gain[...]
        bias_ref[...] = bias[...]

    row = shaped(1, channels)
    held = jax.ShapeDtypeStruct(weight_one.shape, weight_one.dtype)
    weight_one, weight_two, gain, bias = call(
        stage, [held, held, row, row], 0, weight_one, weight_two, norm_gain[None], norm_bias[None]
    )
    feats = shifted_copies(features[0], RATE_ONE, ("lon", "lat"))

    def first_conv(s0, s1, s2, weight, pre_ref, stat_ref):
        pre = convolved((s0, s1, s2), weight, step_one, cells, False)
        near = jnp.sum(pre, axis=0, keepdims=True) * (1.0 / cells)
        around = jnp.sum((pre - near) ** 2, axis=0, keepdims=True)
        pre_ref[...] = pre
        stat_ref[...] = jnp.broadcast_to(jnp.concatenate([near, around])[None], stat_ref.shape)

    members = lax.axis_size(TILE)
    copies = jax.ShapeDtypeStruct((members, 2, channels), jnp.float32)
    pre_one, stat = call(first_conv, [shaped(cells, channels), copies], work, *feats, weight_one)
    stats = lax.all_to_all(stat, TILE, 0, 0)

    cotan = shifted_copies(out_cotangent[0], RATE_TWO, ("lon", "lat"))

    def cotangent_conv(c0, c1, c2, weight, out_ref):
        out_ref[...] = convolved((c0, c1, c2), weight, step_two, cells, True)

    (grad_hidden,) = call(cotangent_conv, [shaped(cells, channels)], work, *cotan, weight_two)

    def activate(stats, pre, grad, gain, bias, hidden_ref, shift_ref, normed_ref, rstd_ref, sums_ref):
        means = stats[:, 0, :]
        mean = jnp.sum(means, axis=0, keepdims=True) * (1.0 / members)
        apart = jnp.sum((means - mean) ** 2, axis=0, keepdims=True)
        var = (jnp.sum(stats[:, 1, :], axis=0, keepdims=True) + cells * apart) * (1.0 / count)
        rstd = lax.rsqrt(var + 1e-05)
        normed = (pre[...] - mean) * rstd
        shifted = gain[...] * normed + bias[...]
        sig = 1.0 / (1.0 + jnp.exp(-shifted))
        hidden_ref[...] = (shifted * sig).astype(jnp.bfloat16)
        shift = grad[...] * sig * (1.0 + shifted * (1.0 - sig))
        shift_ref[...] = shift
        normed_ref[...] = normed
        rstd_ref[...] = rstd
        sum_b = jnp.sum(shift, axis=0, keepdims=True)
        sum_ba = jnp.sum(shift * normed, axis=0, keepdims=True)
        sums_ref[...] = jnp.broadcast_to(jnp.concatenate([sum_b, sum_ba])[None], sums_ref.shape)

    hidden, grad_shift, normed, rstd, sums = call(
        activate,
        [
            shaped(cells, channels, jnp.bfloat16),
            shaped(cells, channels),
            shaped(cells, channels),
            row,
            copies,
        ],
        cells * channels * 20,
        stats, pre_one, grad_hidden, gain, bias,
    )
    every = lax.all_to_all(sums, TILE, 0, 0)

    hiddens = shifted_copies(hidden.reshape(rows, cols, channels), RATE_TWO, ("lat", "lon"))

    def second_conv(h0, h1, h2, weight, out_ref):
        out_ref[...] = convolved((h0, h1, h2), weight, step_two, cells, False).astype(jnp.bfloat16)

    def second_grad(hidden, c0, c1, c2, out_ref):
        for n, (a, b) in enumerate(TAPS):
            window = (c0, c1, c2)[2 - b][(2 - a) * step_two : (2 - a) * step_two + cells, :]
            out_ref[n * channels : (n + 1) * channels, :] = dot(hidden[...], window, (0, 0)).astype(jnp.bfloat16)

    part_shape = shaped(9 * channels, channels, jnp.bfloat16)
    (part_two,) = call(second_grad, [part_shape], work, hidden, *cotan)

    def first_grad(every, shift, normed, gain, rstd, s0, s1, s2, out_ref, own_ref):
        scale = gain[...] * rstd[...]
        own = jnp.sum(every[...], axis=0)
        own_ref[...] = own
        base = own[0:1, :] * (1.0 / count)
        slope = own[1:2, :] * (1.0 / count)
        grad = ((shift[...] - base - normed[...] * slope) * scale).astype(jnp.bfloat16)
        for n, (a, b) in enumerate(TAPS):
            window = (s0, s1, s2)[b][a * step_one : a * step_one + cells, :]
            out_ref[n * channels : (n + 1) * channels, :] = dot(window, grad, (0, 0)).astype(jnp.bfloat16)

    part_one, own = call(first_grad, [part_shape, shaped(2, channels)], work, every, grad_shift, normed, gain, rstd, *feats)

    lon, lat, batch = (lax.axis_size(a) for a in EVERY)
    both = own
    for shift in range(1, batch):
        both = both + lax.ppermute(own, "batch", [(i, (i + shift) % batch) for i in range(batch)])
    grad_bias, grad_gain = both
    pairs = [(i, i ^ 1) for i in range(lon)]
    core = lax.axis_index("lon") % 2 == 1
    groups = [
        [((x * 2 + c) * lat + z) * batch + y for x in range(lon // 2) for z in range(lat) for y in range(batch)]
        for c in range(2)
    ]
    size = lon * lat * batch // 2
    total = 9 * channels
    chunk = -(-total // (size * 8)) * 8
    sent = jnp.where(core, part_one, part_two)
    kept = jnp.where(core, part_two, part_one)
    arrived = lax.ppermute(sent, "lon", pairs)
    half = (kept.astype(jnp.float32) + arrived.astype(jnp.float32)).astype(jnp.bfloat16)
    half = jnp.pad(half, ((0, chunk * size - total), (0, 0)))
    chunks = lax.all_to_all(half.reshape(size, chunk, channels), EVERY, 0, 0, axis_index_groups=groups)
    piece = jnp.sum(chunks.astype(jnp.float32), axis=0).astype(jnp.bfloat16)
    whole = lax.all_to_all(
        jnp.broadcast_to(piece[None], (size, chunk, channels)), EVERY, 0, 0, axis_index_groups=groups
    )
    (maps,) = call(second_conv, [shaped(cells, channels, jnp.bfloat16)], work, *hiddens, weight_two)
    mine = whole.reshape(size * chunk, channels)[:total]
    other = lax.ppermute(mine, "lon", pairs)
    odd = core.astype(jnp.int32).reshape(1, 1)

    def emit(odd, mine, other, one_ref, two_ref):
        swap = jnp.broadcast_to(odd[...], (8, channels)) == 1

        def body(i, _):
            at = pl.ds(pl.multiple_of(i * channels, channels), channels)
            a, b = mine[at, :].astype(jnp.float32), other[at, :].astype(jnp.float32)
            pick = jnp.broadcast_to(swap[:1], (channels, channels))
            one_ref[at, :] = jnp.where(pick, b, a)
            two_ref[at, :] = jnp.where(pick, a, b)
            return 0

        lax.fori_loop(0, 9, body, 0)

    grad_one, grad_two = call(emit, [shaped(total, channels)] * 2, 0, odd, mine, other)
    shape = weight_one.shape
    grad_one, grad_two = grad_one.reshape(shape), grad_two.reshape(shape)
    return (maps.reshape(features.shape), grad_one, grad_two, grad_gain, grad_bias)


def solution(mesh):
    placed = (P("batch", "lon", "lat", None), P(), P(), P(), P(), P("batch", "lon", "lat", None))

    return jax.shard_map(
        local,
        mesh=mesh,
        in_specs=placed,
        out_specs=(P("batch", "lon", "lat", None), P(), P(), P(), P()),
        check_vma=False,
    )
```

```python
import jax
import jax.numpy as jnp
from jax import lax
from jax.experimental import pallas as pl
from jax.experimental.pallas import tpu as pltpu
from jax.sharding import PartitionSpec as P


RATE_ONE = 6
RATE_TWO = 12
TILE = ("lon", "lat")
EVERY = ("lon", "lat", "batch")
TAPS = [(a, b) for a in range(3) for b in range(3)]
LIMIT = 32 * 1024 * 1024


def swapped(first, last, axis, wrap):
    devices = lax.axis_size(axis)
    odd = lax.axis_index(axis) % 2 == 1
    near = [(i, i ^ 1) for i in range(devices)]
    far = [(i, (i + 1 if i % 2 else i - 1) % devices) for i in range(devices)]
    if not wrap:
        far = [(i, j) for i, j in far if abs(i - j) == 1]
    one = lax.ppermute(jnp.where(odd, first, last), axis, near)
    two = lax.ppermute(jnp.where(odd, last, first), axis, far)
    return jnp.where(odd, one, two), jnp.where(odd, two, one)


def widened(tile, width, axis):
    dim = ("lon", "lat").index(axis)
    length = tile.shape[dim]
    first = lax.slice_in_dim(tile, 0, width, axis=dim)
    last = lax.slice_in_dim(tile, length - width, length, axis=dim)
    before, after = swapped(first, last, axis, axis == "lon")
    return jnp.concatenate([before, tile, after], axis=dim)


def shifts(wide, width):
    cols = wide.shape[1] - 2 * width
    return [wide[:, b * width : b * width + cols].reshape(-1, wide.shape[2]) for b in range(3)]


def shifted_copies(tile, width, order):
    for axis in order:
        tile = widened(tile, width, axis)
    return shifts(tile, width)


def members_of(keep):
    lon, lat, batch = (lax.axis_size(a) for a in EVERY)
    middle = sorted(range(lat), key=lambda z: abs(2 * z + 1 - lat))
    found = {}
    for x in reversed(range(lon)):
        for z in middle:
            for y in range(batch):
                found.setdefault(keep(x, y), []).append((x * lat + z) * batch + y)
    return list(found.values())


def call(body, outs, flops, *args):
    moved = sum(a.size * a.dtype.itemsize for a in args) + sum(o.size * o.dtype.itemsize for o in outs)
    return pl.pallas_call(
        body,
        out_shape=outs,
        compiler_params=pltpu.CompilerParams(vmem_limit_bytes=LIMIT),
        cost_estimate=pl.CostEstimate(flops=flops, bytes_accessed=moved, transcendentals=0),
    )(*args)


def shaped(rows, channels, kind=jnp.float32):
    return jax.ShapeDtypeStruct((rows, channels), kind)


def dot(left, right, over):
    return lax.dot_general(left, right, ((over[:1], over[1:]), ((), ())), preferred_element_type=jnp.float32)


def convolved(shifts, weight, step, cells, flip):
    total = None
    for a, b in TAPS:
        kernel = weight[2 - a, 2 - b] if flip else weight[a, b]
        term = dot(shifts[b][a * step : a * step + cells, :], kernel, (1, 1) if flip else (1, 0))
        total = term if total is None else total + term
    return total


def local(features, weight_one, norm_gain, norm_bias, weight_two, out_cotangent):
    _, rows, cols, channels = features.shape
    cells = rows * cols
    count = cells * lax.axis_size(TILE)
    step_one, step_two = RATE_ONE * cols, RATE_TWO * cols
    work = 2 * 9 * cells * channels * channels

    def stage(w1, w2, gain, bias, w1_ref, w2_ref, gain_ref, bias_ref):
        w1_ref[...] = w1[...]
        w2_ref[...] = w2[...]
        gain_ref[...] = gain[...]
        bias_ref[...] = bias[...]

    row = shaped(1, channels)
    held = jax.ShapeDtypeStruct(weight_one.shape, weight_one.dtype)
    weight_one, weight_two, gain, bias = call(
        stage, [held, held, row, row], 0, weight_one, weight_two, norm_gain[None], norm_bias[None]
    )
    feats = shifted_copies(features[0], RATE_ONE, ("lon", "lat"))

    def first_conv(s0, s1, s2, weight, pre_ref, stat_ref):
        pre = convolved((s0, s1, s2), weight, step_one, cells, False)
        near = jnp.sum(pre, axis=0, keepdims=True) * (1.0 / cells)
        around = jnp.sum((pre - near) ** 2, axis=0, keepdims=True)
        pre_ref[...] = pre
        stat_ref[...] = jnp.broadcast_to(jnp.concatenate([near, around])[None], stat_ref.shape)

    members = lax.axis_size(TILE)
    tile = members_of(lambda x, y: y)
    copies = jax.ShapeDtypeStruct((members, 2, channels), jnp.float32)
    pre_one, stat = call(first_conv, [shaped(cells, channels), copies], work, *feats, weight_one)
    stats = lax.all_to_all(stat, EVERY, 0, 0, axis_index_groups=tile)

    cotan = shifted_copies(out_cotangent[0], RATE_TWO, ("lon", "lat"))

    def cotangent_conv(c0, c1, c2, weight, out_ref):
        out_ref[...] = convolved((c0, c1, c2), weight, step_two, cells, True)

    (grad_hidden,) = call(cotangent_conv, [shaped(cells, channels)], work, *cotan, weight_two)

    def activate(stats, pre, grad, gain, bias, hidden_ref, shift_ref, normed_ref, rstd_ref, sums_ref):
        means = stats[:, 0, :]
        mean = jnp.sum(means, axis=0, keepdims=True) * (1.0 / members)
        apart = jnp.sum((means - mean) ** 2, axis=0, keepdims=True)
        var = (jnp.sum(stats[:, 1, :], axis=0, keepdims=True) + cells * apart) * (1.0 / count)
        rstd = lax.rsqrt(var + 1e-05)
        normed = (pre[...] - mean) * rstd
        shifted = gain[...] * normed + bias[...]
        sig = 1.0 / (1.0 + jnp.exp(-shifted))
        hidden_ref[...] = (shifted * sig).astype(jnp.bfloat16)
        shift = grad[...] * sig * (1.0 + shifted * (1.0 - sig))
        shift_ref[...] = shift
        normed_ref[...] = normed
        rstd_ref[...] = rstd
        sum_b = jnp.sum(shift, axis=0, keepdims=True)
        sum_ba = jnp.sum(shift * normed, axis=0, keepdims=True)
        sums_ref[...] = jnp.broadcast_to(jnp.concatenate([sum_b, sum_ba])[None], sums_ref.shape)

    hidden, grad_shift, normed, rstd, sums = call(
        activate,
        [
            shaped(cells, channels, jnp.bfloat16),
            shaped(cells, channels),
            shaped(cells, channels),
            row,
            copies,
        ],
        cells * channels * 20,
        stats, pre_one, grad_hidden, gain, bias,
    )
    every = lax.all_to_all(sums, EVERY, 0, 0, axis_index_groups=tile)

    hiddens = shifted_copies(hidden.reshape(rows, cols, channels), RATE_TWO, ("lat", "lon"))

    def second_conv(h0, h1, h2, weight, out_ref):
        out_ref[...] = convolved((h0, h1, h2), weight, step_two, cells, False).astype(jnp.bfloat16)

    def second_grad(hidden, c0, c1, c2, out_ref):
        for n, (a, b) in enumerate(TAPS):
            window = (c0, c1, c2)[2 - b][(2 - a) * step_two : (2 - a) * step_two + cells, :]
            out_ref[n * channels : (n + 1) * channels, :] = dot(hidden[...], window, (0, 0)).astype(jnp.bfloat16)

    part_shape = shaped(9 * channels, channels, jnp.bfloat16)
    (part_two,) = call(second_grad, [part_shape], work, hidden, *cotan)

    def first_grad(every, shift, normed, gain, rstd, s0, s1, s2, out_ref, own_ref):
        scale = gain[...] * rstd[...]
        own = jnp.sum(every[...], axis=0)
        own_ref[...] = own
        base = own[0:1, :] * (1.0 / count)
        slope = own[1:2, :] * (1.0 / count)
        grad = ((shift[...] - base - normed[...] * slope) * scale).astype(jnp.bfloat16)
        for n, (a, b) in enumerate(TAPS):
            window = (s0, s1, s2)[b][a * step_one : a * step_one + cells, :]
            out_ref[n * channels : (n + 1) * channels, :] = dot(window, grad, (0, 0)).astype(jnp.bfloat16)

    part_one, own = call(first_grad, [part_shape, shaped(2, channels)], work, every, grad_shift, normed, gain, rstd, *feats)

    lon, lat, batch = (lax.axis_size(a) for a in EVERY)
    both = own
    for shift in range(1, batch):
        both = both + lax.ppermute(own, "batch", [(i, (i + shift) % batch) for i in range(batch)])
    grad_bias, grad_gain = both
    pairs = [(i, i ^ 1) for i in range(lon)]
    core = lax.axis_index("lon") % 2 == 1
    groups = members_of(lambda x, y: x % 2)
    size = lon * lat * batch // 2
    total = 9 * channels
    chunk = -(-total // (size * 8)) * 8
    sent = jnp.where(core, part_one, part_two)
    kept = jnp.where(core, part_two, part_one)
    arrived = lax.ppermute(sent, "lon", pairs)
    half = (kept.astype(jnp.float32) + arrived.astype(jnp.float32)).astype(jnp.bfloat16)
    half = jnp.pad(half, ((0, chunk * size - total), (0, 0)))
    chunks = lax.all_to_all(half.reshape(size, chunk, channels), EVERY, 0, 0, axis_index_groups=groups)
    piece = jnp.sum(chunks.astype(jnp.float32), axis=0).astype(jnp.bfloat16)
    whole = lax.all_to_all(
        jnp.broadcast_to(piece[None], (size, chunk, channels)), EVERY, 0, 0, axis_index_groups=groups
    )
    (maps,) = call(second_conv, [shaped(cells, channels, jnp.bfloat16)], work, *hiddens, weight_two)
    mine = whole.reshape(size * chunk, channels)[:total]
    other = lax.ppermute(mine, "lon", pairs)
    odd = core.astype(jnp.int32).reshape(1, 1)

    def emit(odd, mine, other, one_ref, two_ref):
        swap = jnp.broadcast_to(odd[...], (8, channels)) == 1

        def body(i, _):
            at = pl.ds(pl.multiple_of(i * channels, channels), channels)
            a, b = mine[at, :].astype(jnp.float32), other[at, :].astype(jnp.float32)
            pick = jnp.broadcast_to(swap[:1], (channels, channels))
            one_ref[at, :] = jnp.where(pick, b, a)
            two_ref[at, :] = jnp.where(pick, a, b)
            return 0

        lax.fori_loop(0, 9, body, 0)

    grad_one, grad_two = call(emit, [shaped(total, channels)] * 2, 0, odd, mine, other)
    shape = weight_one.shape
    grad_one, grad_two = grad_one.reshape(shape), grad_two.reshape(shape)
    return (maps.reshape(features.shape), grad_one, grad_two, grad_gain, grad_bias)


def solution(mesh):
    placed = (P("batch", "lon", "lat", None), P(), P(), P(), P(), P("batch", "lon", "lat", None))

    return jax.shard_map(
        local,
        mesh=mesh,
        in_specs=placed,
        out_specs=(P("batch", "lon", "lat", None), P(), P(), P(), P()),
        check_vma=False,
    )
```

```python
import jax
import jax.numpy as jnp
from jax import lax
from jax.experimental import pallas as pl
from jax.experimental.pallas import tpu as pltpu
from jax.sharding import PartitionSpec as P


RATE_ONE = 6
RATE_TWO = 12
TILE = ("lon", "lat")
EVERY = ("lon", "lat", "batch")
TAPS = [(a, b) for a in range(3) for b in range(3)]
LIMIT = 32 * 1024 * 1024


def swapped(first, last, axis, wrap):
    devices = lax.axis_size(axis)
    odd = lax.axis_index(axis) % 2 == 1
    near = [(i, i ^ 1) for i in range(devices)]
    far = [(i, (i + 1 if i % 2 else i - 1) % devices) for i in range(devices)]
    if not wrap:
        far = [(i, j) for i, j in far if abs(i - j) == 1]
    one = lax.ppermute(jnp.where(odd, first, last), axis, near)
    two = lax.ppermute(jnp.where(odd, last, first), axis, far)
    return jnp.where(odd, one, two), jnp.where(odd, two, one)


def widened(tile, width, axis):
    dim = ("lon", "lat").index(axis)
    length = tile.shape[dim]
    first = lax.slice_in_dim(tile, 0, width, axis=dim)
    last = lax.slice_in_dim(tile, length - width, length, axis=dim)
    before, after = swapped(first, last, axis, axis == "lon")
    return jnp.concatenate([before, tile, after], axis=dim)


def shifts(wide, width):
    cols = wide.shape[1] - 2 * width
    return [wide[:, b * width : b * width + cols].reshape(-1, wide.shape[2]) for b in range(3)]


def shifted_copies(tile, width, order):
    for axis in order:
        tile = widened(tile, width, axis)
    return shifts(tile, width)


def members_of(keep):
    lon, lat, batch = (lax.axis_size(a) for a in EVERY)
    middle = sorted(range(lat), key=lambda z: abs(2 * z + 1 - lat))
    found = {}
    for y in range(batch):
        for x in reversed(range(lon)):
            for z in middle:
                found.setdefault(keep(x, y), []).append((x * lat + z) * batch + y)
    return list(found.values())


def call(body, outs, flops, *args):
    moved = sum(a.size * a.dtype.itemsize for a in args) + sum(o.size * o.dtype.itemsize for o in outs)
    return pl.pallas_call(
        body,
        out_shape=outs,
        compiler_params=pltpu.CompilerParams(vmem_limit_bytes=LIMIT),
        cost_estimate=pl.CostEstimate(flops=flops, bytes_accessed=moved, transcendentals=0),
    )(*args)


def shaped(rows, channels, kind=jnp.float32):
    return jax.ShapeDtypeStruct((rows, channels), kind)


def dot(left, right, over):
    return lax.dot_general(left, right, ((over[:1], over[1:]), ((), ())), preferred_element_type=jnp.float32)


def convolved(shifts, weight, step, cells, flip):
    total = None
    for a, b in TAPS:
        kernel = weight[2 - a, 2 - b] if flip else weight[a, b]
        term = dot(shifts[b][a * step : a * step + cells, :], kernel, (1, 1) if flip else (1, 0))
        total = term if total is None else total + term
    return total


def local(features, weight_one, norm_gain, norm_bias, weight_two, out_cotangent):
    _, rows, cols, channels = features.shape
    cells = rows * cols
    count = cells * lax.axis_size(TILE)
    step_one, step_two = RATE_ONE * cols, RATE_TWO * cols
    work = 2 * 9 * cells * channels * channels

    row = shaped(1, channels)
    gain, bias = norm_gain[None], norm_bias[None]
    feats = shifted_copies(features[0], RATE_ONE, ("lon", "lat"))

    def first_conv(s0, s1, s2, weight, pre_ref, stat_ref):
        pre = convolved((s0, s1, s2), weight, step_one, cells, False)
        near = jnp.sum(pre, axis=0, keepdims=True) * (1.0 / cells)
        around = jnp.sum((pre - near) ** 2, axis=0, keepdims=True)
        pre_ref[...] = pre
        stat_ref[...] = jnp.broadcast_to(jnp.concatenate([near, around])[None], stat_ref.shape)

    members = lax.axis_size(TILE)
    tile = members_of(lambda x, y: y)
    copies = jax.ShapeDtypeStruct((members, 2, channels), jnp.float32)
    pre_one, stat = call(first_conv, [shaped(cells, channels), copies], work, *feats, weight_one)
    stats = lax.all_to_all(stat, EVERY, 0, 0, axis_index_groups=tile)

    cotan = shifted_copies(out_cotangent[0], RATE_TWO, ("lon", "lat"))

    def cotangent_conv(c0, c1, c2, weight, out_ref):
        out_ref[...] = convolved((c0, c1, c2), weight, step_two, cells, True)

    (grad_hidden,) = call(cotangent_conv, [shaped(cells, channels)], work, *cotan, weight_two)

    def activate(stats, pre, grad, gain, bias, hidden_ref, shift_ref, normed_ref, rstd_ref, sums_ref):
        means = stats[:, 0, :]
        mean = jnp.sum(means, axis=0, keepdims=True) * (1.0 / members)
        apart = jnp.sum((means - mean) ** 2, axis=0, keepdims=True)
        var = (jnp.sum(stats[:, 1, :], axis=0, keepdims=True) + cells * apart) * (1.0 / count)
        rstd = lax.rsqrt(var + 1e-05)
        normed = (pre[...] - mean) * rstd
        shifted = gain[...] * normed + bias[...]
        sig = 1.0 / (1.0 + jnp.exp(-shifted))
        hidden_ref[...] = (shifted * sig).astype(jnp.bfloat16)
        shift = grad[...] * sig * (1.0 + shifted * (1.0 - sig))
        shift_ref[...] = shift
        normed_ref[...] = normed
        rstd_ref[...] = rstd
        sum_b = jnp.sum(shift, axis=0, keepdims=True)
        sum_ba = jnp.sum(shift * normed, axis=0, keepdims=True)
        sums_ref[...] = jnp.broadcast_to(jnp.concatenate([sum_b, sum_ba])[None], sums_ref.shape)

    hidden, grad_shift, normed, rstd, sums = call(
        activate,
        [
            shaped(cells, channels, jnp.bfloat16),
            shaped(cells, channels),
            shaped(cells, channels),
            row,
            copies,
        ],
        cells * channels * 20,
        stats, pre_one, grad_hidden, gain, bias,
    )
    every = lax.all_to_all(sums, EVERY, 0, 0, axis_index_groups=tile)

    hiddens = shifted_copies(hidden.reshape(rows, cols, channels), RATE_TWO, ("lat", "lon"))

    def second_conv(h0, h1, h2, weight, out_ref):
        out_ref[...] = convolved((h0, h1, h2), weight, step_two, cells, False).astype(jnp.bfloat16)

    def second_grad(hidden, c0, c1, c2, out_ref):
        for n, (a, b) in enumerate(TAPS):
            window = (c0, c1, c2)[2 - b][(2 - a) * step_two : (2 - a) * step_two + cells, :]
            out_ref[n * channels : (n + 1) * channels, :] = dot(hidden[...], window, (0, 0)).astype(jnp.bfloat16)

    part_shape = shaped(9 * channels, channels, jnp.bfloat16)
    (part_two,) = call(second_grad, [part_shape], work, hidden, *cotan)

    def first_grad(every, shift, normed, gain, rstd, s0, s1, s2, out_ref, own_ref):
        scale = gain[...] * rstd[...]
        own = jnp.sum(every[...], axis=0)
        own_ref[...] = own
        base = own[0:1, :] * (1.0 / count)
        slope = own[1:2, :] * (1.0 / count)
        grad = ((shift[...] - base - normed[...] * slope) * scale).astype(jnp.bfloat16)
        for n, (a, b) in enumerate(TAPS):
            window = (s0, s1, s2)[b][a * step_one : a * step_one + cells, :]
            out_ref[n * channels : (n + 1) * channels, :] = dot(window, grad, (0, 0)).astype(jnp.bfloat16)

    part_one, own = call(first_grad, [part_shape, shaped(2, channels)], work, every, grad_shift, normed, gain, rstd, *feats)

    lon, lat, batch = (lax.axis_size(a) for a in EVERY)
    both = own
    for shift in range(1, batch):
        both = both + lax.ppermute(own, "batch", [(i, (i + shift) % batch) for i in range(batch)])
    grad_bias, grad_gain = both
    pairs = [(i, i ^ 1) for i in range(lon)]
    core = lax.axis_index("lon") % 2 == 1
    groups = members_of(lambda x, y: x % 2)
    size = lon * lat * batch // 2
    total = 9 * channels
    chunk = -(-total // (size * 8)) * 8
    sent = jnp.where(core, part_one, part_two)
    kept = jnp.where(core, part_two, part_one)
    arrived = lax.ppermute(sent, "lon", pairs)
    half = (kept.astype(jnp.float32) + arrived.astype(jnp.float32)).astype(jnp.bfloat16)
    half = jnp.pad(half, ((0, chunk * size - total), (0, 0)))
    chunks = lax.all_to_all(half.reshape(size, chunk, channels), EVERY, 0, 0, axis_index_groups=groups)
    piece = jnp.sum(chunks.astype(jnp.float32), axis=0).astype(jnp.bfloat16)
    whole = lax.all_to_all(
        jnp.broadcast_to(piece[None], (size, chunk, channels)), EVERY, 0, 0, axis_index_groups=groups
    )
    (maps,) = call(second_conv, [shaped(cells, channels, jnp.bfloat16)], work, *hiddens, weight_two)
    mine = whole.reshape(size * chunk, channels)[:total]
    other = lax.ppermute(mine, "lon", pairs)
    odd = core.astype(jnp.int32).reshape(1, 1)

    def emit(odd, mine, other, one_ref, two_ref, one_buf, two_buf, sems):
        swap = jnp.broadcast_to(odd[...], (channels, channels)) == 1
        sent = []
        for part in range(3):
            for n in range(3 * part, 3 * part + 3):
                at = slice(n * channels, (n + 1) * channels)
                a, b = mine[at, :].astype(jnp.float32), other[at, :].astype(jnp.float32)
                one_buf[at, :] = jnp.where(swap, b, a)
                two_buf[at, :] = jnp.where(swap, a, b)
            span = pl.ds(3 * part * channels, 3 * channels)
            for k, (buf, ref) in enumerate(((one_buf, one_ref), (two_buf, two_ref))):
                sent.append(pltpu.make_async_copy(buf.at[span], ref.at[span], sems.at[k, part]))
                sent[-1].start()
        for copy in sent:
            copy.wait()

    grad_one, grad_two = pl.pallas_call(
        emit,
        out_shape=[shaped(total, channels)] * 2,
        in_specs=[pl.BlockSpec(memory_space=pltpu.VMEM)] * 3,
        out_specs=[pl.BlockSpec(memory_space=pl.ANY)] * 2,
        scratch_shapes=[pltpu.VMEM((total, channels), jnp.float32)] * 2 + [pltpu.SemaphoreType.DMA((2, 3))],
        compiler_params=pltpu.CompilerParams(vmem_limit_bytes=LIMIT),
        name="emit",
    )(odd, mine, other)
    shape = weight_one.shape
    grad_one, grad_two = grad_one.reshape(shape), grad_two.reshape(shape)
    return (maps.reshape(features.shape), grad_one, grad_two, grad_gain, grad_bias)


def solution(mesh):
    placed = (P("batch", "lon", "lat", None), P(), P(), P(), P(), P("batch", "lon", "lat", None))

    return jax.shard_map(
        local,
        mesh=mesh,
        in_specs=placed,
        out_specs=(P("batch", "lon", "lat", None), P(), P(), P(), P()),
        check_vma=False,
    )
```
